32 devices in a mesh: dp: 16 (over z, y, core), grp: 2 (over x).
Axes of the slice: x: 2, y: 2, z: 4, core: 2. Of those that a mesh axis runs over, the one named last changes fastest.
Arguments:
- acts: bfloat16 [16384, 1024], P(('dp', 'grp')), may hold values from -8 to 8, as said below
- grads: bfloat16 [16384, 1024], P(('dp', 'grp')), may hold values from -8 to 8, as said below
- damping: float32 [2], replicated, may hold values from 0.02 to 0.2
Outputs:
- preconditioned: float32 [1024, 1024], P('dp', 'grp')
The draws below stay inside these ranges and needn't reach their ends.
Inputs may be any that keep to these rules, and one draw needn't show every extreme that they name: `acts`: activations of one token are correlated across features. `grads`: output gradients are correlated with the activations.
All inputs are finite; a program needn't handle non-finite values. Where the reference program divides by a largest or mean magnitude, that divisor is 1e-20 or more.
Results may differ from the reference program's by a relative error of at most 0.0003.
Values sent between devices are 32-bit elements; how exact they have to be, the bound alone decides.
A program may use at most 64 MiB of HBM per device.

```python
import math
import jax
import jax.numpy as jnp
from jax import lax

D = 1024
ITERS = 4
TOKENS = 16384


def base_acts(key):
    inner = jax.random.fold_in(key, 101)
    key_noise, key_mix, key_scale = jax.random.split(inner, 3)
    noise = jax.random.normal(key_noise, (TOKENS, D), jnp.float32)
    mixing = jnp.eye(D, dtype=jnp.float32) + 0.5 * jax.random.normal(key_mix, (D, D), jnp.float32) / math.sqrt(D)
    scales = jnp.exp(jax.random.uniform(key_scale, (D,), jnp.float32, math.log(0.1), 0.0))
    return jnp.dot(noise, mixing, precision=lax.Precision.HIGHEST) * scales


def draw_acts(key, part):
    return jnp.clip(base_acts(key), -8.0, 8.0).astype(jnp.bfloat16)


def draw_grads(key, part):
    values = base_acts(key)
    inner = jax.random.fold_in(key, 202)
    key_cross, key_noise, key_scale = jax.random.split(inner, 3)
    coupling = jax.random.normal(key_cross, (D, D), jnp.float32) / math.sqrt(D)
    noise = jax.random.normal(key_noise, (TOKENS, D), jnp.float32)
    scales = jnp.exp(jax.random.uniform(key_scale, (D,), jnp.float32, math.log(0.1), 0.0))
    result = jnp.dot(values, coupling, precision=lax.Precision.HIGHEST) + noise * scales
    return jnp.clip(result, -8.0, 8.0).astype(jnp.bfloat16)


def setup_inputs(seed: int = 0) -> dict:
    key_of = jax.random.split(jax.random.key(seed), 4)
    return {
        "acts": draw_acts(jax.random.fold_in(key_of[3], 71), 0),
        "grads": draw_grads(jax.random.fold_in(key_of[3], 71), 0),
        "damping": jnp.clip(jnp.exp(jax.random.uniform(key_of[2], (2,), jnp.float32, math.log(0.02), math.log(0.2))), 0.02, 0.2),
    }


def newton_inverse(gram, damp):
    size = gram.shape[0]
    eye = jnp.eye(size, dtype=jnp.float32)
    matrix = gram + damp * eye
    alpha = 1.0 / jnp.max(jnp.sum(jnp.abs(matrix), axis=1))
    iterate = alpha * eye
    for step in range(ITERS):
        image = jnp.dot(matrix, iterate, precision=lax.Precision.HIGHEST)
        iterate = 2.0 * iterate - jnp.dot(iterate, image, precision=lax.Precision.HIGHEST)
    return iterate


def reference(acts, grads, damping):
    contract = (((0,), (0,)), ((), ()))
    scale = 1.0 / TOKENS
    gram_acts = lax.dot_general(acts, acts, contract, preferred_element_type=jnp.float32) * scale
    gram_grads = lax.dot_general(grads, grads, contract, preferred_element_type=jnp.float32) * scale
    left = newton_inverse(gram_acts, damping[0])
    right = newton_inverse(gram_grads, damping[1])
    mapped = jnp.dot(acts.astype(jnp.float32), left, precision=lax.Precision.HIGHEST)
    weighted = jnp.dot(grads.astype(jnp.float32), right, precision=lax.Precision.HIGHEST)
    return lax.dot_general(mapped, weighted, contract, precision=lax.Precision.HIGHEST, preferred_element_type=jnp.float32) * scale
```

```python
import jax
import jax.numpy as jnp
from jax import lax
from jax.sharding import PartitionSpec as P


def product(left, right):
    return jnp.dot(left, right, precision=lax.Precision.HIGH, preferred_element_type=jnp.float32)


def factors(matrix):
    alpha = 1.0 / jnp.max(jnp.sum(jnp.abs(matrix), axis=1))
    first = jnp.eye(matrix.shape[0], dtype=jnp.float32) - alpha * matrix
    second = product(first, first)
    return alpha, first, second, product(second, second)


def apply_inverse(block, parts):
    alpha, first, second, fourth = parts
    block = block + product(block, first)
    block = block + product(block, second)
    block = block + product(block, fourth)
    return alpha * (block + product(product(block, fourth), fourth))


def local(acts, grads, damping):
    dp_size = lax.axis_size("dp")
    grp_size = lax.axis_size("grp")
    width = acts.shape[1]
    scale = 1.0 / (acts.shape[0] * dp_size * grp_size)
    contract = (((0,), (0,)), ((), ()))

    def gram(left, right):
        return lax.dot_general(left, right, contract, preferred_element_type=jnp.float32) * scale

    terms = jnp.stack([gram(acts, acts), gram(grads, grads), gram(grads, acts)])
    rows = lax.psum_scatter(terms, "dp", scatter_dimension=1, tiled=True)
    rows = lax.psum_scatter(rows, "grp", scatter_dimension=1, tiled=True)
    grams = lax.all_gather(rows[:2], ("dp", "grp"), axis=1, tiled=True)
    eye = jnp.eye(width, dtype=jnp.float32)
    left = factors(grams[0] + damping[0] * eye)
    right = factors(grams[1] + damping[1] * eye)
    mapped = apply_inverse(rows[2], left).T
    mapped = lax.all_to_all(mapped, ("dp", "grp"), 0, 1, tiled=True)
    result = apply_inverse(mapped, right)
    return lax.all_to_all(result, "grp", 1, 0, tiled=True)


def solution(mesh):
    placed = (P(("dp", "grp"), None), P(("dp", "grp"), None), P())
    return jax.shard_map(
        local, mesh=mesh, in_specs=placed, out_specs=P("dp", "grp"), check_vma=False
    )
```

```python
import functools

import jax
import jax.numpy as jnp
from jax import lax
from jax.experimental import pallas as pl
from jax.experimental.pallas import tpu as pltpu
from jax.sharding import PartitionSpec as P

LANES = 256
MESH = pl.DeviceIdType.MESH


def product(left, right):
    return jnp.dot(left, right, precision=lax.Precision.HIGH, preferred_element_type=jnp.float32)


def factors(matrix):
    alpha = 1.0 / jnp.max(jnp.sum(jnp.abs(matrix), axis=1))
    first = jnp.eye(matrix.shape[0], dtype=jnp.float32) - alpha * matrix
    second = product(first, first)
    return alpha, first, second, product(second, second)


def apply_inverse(block, parts):
    alpha, first, second, fourth = parts
    block = block + product(block, first)
    block = block + product(block, second)
    block = block + product(block, fourth)
    return alpha * (block + product(product(block, fourth), fourth))


def reduce_kernel(
    nz, nx, acts, grads, mat, cross,
    stack, flipped, outgoing, incoming, own,
    sum_e, sum_o, got_e1, got_e2, got_o1, got_o2, pair, got_z, mine,
    send_sem, recv_sem,
):
    dp = lax.axis_index("dp")
    x = lax.axis_index("grp")
    core = lax.rem(dp, 2)
    y = lax.rem(dp // 2, 2)
    z = dp // 4
    other = 1 - core
    width = acts.shape[1]
    n_mat = width // LANES
    n_all = n_mat + width // 2 // LANES
    half = width // 2

    def at(zz, yy, cc, xx):
        return ((zz * 2 + yy) * 2 + cc, xx)

    partner = at(z, y, other, x)
    y_peer = at(z, 1 - y, core, x)
    x_ids = [lax.rem(x + o, nx) for o in range(1, nx)]
    z_ids = [lax.rem(z + o, nz) for o in range(1, nz)]
    x_peers = [at(z, y, core, i) for i in x_ids]
    z_peers = [at(i, y, core, x) for i in z_ids]
    peers = [partner, y_peer] + x_peers + z_peers

    barrier = pltpu.get_barrier_semaphore()
    for peer in peers:
        pl.semaphore_signal(barrier, inc=1, device_id=peer, device_id_type=MESH)
    pl.semaphore_wait(barrier, len(peers))

    count = [0]
    copies = []

    def send(src, dst, peer):
        n = count[0]
        count[0] += 1
        copy = pltpu.make_async_remote_copy(
            src_ref=src, dst_ref=dst, send_sem=send_sem.at[n], recv_sem=recv_sem.at[n],
            device_id=peer, device_id_type=MESH,
        )
        copy.start()
        copies.append(copy)
        return copy

    stack[0] = acts[...]
    stack[1] = grads[...]
    flipped[0] = acts[...].T
    flipped[1] = grads[...].T

    def term(role, chunk):
        if chunk < n_mat:
            left = flipped[role]
            right = stack[role, :, chunk * LANES:(chunk + 1) * LANES]
        else:
            start = pl.multiple_of(role * half + (chunk - n_mat) * LANES, LANES)
            left = flipped[1]
            right = stack[0, :, pl.ds(start, LANES)]
        value = jnp.dot(left, right, preferred_element_type=jnp.float32)
        return value.reshape(own.shape[1:])

    waits = {}

    def core_send(c):
        outgoing[c] = term(other, c)
        waits[c] = [send(outgoing.at[c], incoming.at[c], partner)]
        own[c] = term(core, c)

    def arrived(c):
        for copy in waits[c]:
            copy.wait_recv()

    def first(c):
        arrived(c)
        own[c] = own[c] + incoming[c]
        k = c // 2
        if c % 2 == 0:
            waits[c] = [
                send(own.at[c, :, :, i], got_e1.at[k, s], peer)
                for s, (i, peer) in enumerate(zip(x_ids, x_peers))
            ]
        else:
            waits[c] = [send(own.at[c, :, 1 - y], got_o1.at[k], y_peer)]

    def second(c):
        arrived(c)
        k = c // 2
        if c % 2 == 0:
            total = own[c, :, :, x]
            for s in range(nx - 1):
                total = total + got_e1[k, s]
            sum_e[k] = total
            waits[c] = [send(sum_e.at[k, :, 1 - y], got_e2.at[k], y_peer)]
        else:
            sum_o[k] = own[c, :, y] + got_o1[k]
            waits[c] = [
                send(sum_o.at[k, :, i], got_o2.at[k, s], peer)
                for s, (i, peer) in enumerate(zip(x_ids, x_peers))
            ]

    def third(c):
        arrived(c)
        k = c // 2
        if c % 2 == 0:
            pair[c] = sum_e[k, :, y] + got_e2[k]
        else:
            total = sum_o[k, :, x]
            for s in range(nx - 1):
                total = total + got_o2[k, s]
            pair[c] = total
        waits[c] = [
            send(pair.at[c, i], got_z.at[c, s], peer)
            for s, (i, peer) in enumerate(zip(z_ids, z_peers))
        ]

    def fourth(c):
        arrived(c)
        total = pair[c, z]
        for s in range(nz - 1):
            total = total + got_z[c, s]
        mine[c] = total
        if c < n_mat:
            mat[c, z, y, x] = total
            spot = mat.at[c, z, y, x]
            waits[c] = [send(mine.at[c], spot, peer) for peer in z_peers]
        else:
            cross[c - n_mat, core] = total
            waits[c] = [send(mine.at[c], cross.at[c - n_mat, core], partner)]

    def fifth(c):
        arrived(c)
        if c >= n_mat:
            waits[c] = []
        elif c % 2 == 0:
            spot = mat.at[c, :, y, x]
            waits[c] = [send(spot, spot, y_peer)]
        else:
            spot = mat.at[c, :, y, x]
            waits[c] = [send(spot, spot, peer) for peer in x_peers]

    def sixth(c):
        arrived(c)
        if c >= n_mat:
            waits[c] = []
        elif c % 2 == 0:
            spot = mat.at[c, :, :, x]
            waits[c] = [send(spot, spot, peer) for peer in x_peers]
        else:
            spot = mat.at[c, :, y]
            waits[c] = [send(spot, spot, y_peer)]

    steps = [core_send, first, second, third, fourth, fifth, sixth, arrived]
    lag = 2
    for t in range(n_all + lag * len(steps)):
        for s, step in enumerate(steps):
            c = t - lag * s
            if 0 <= c < n_all:
                step(c)
    for copy in copies:
        copy.wait_send()


def reduce_grams(acts, grads, dp_size, grp_size):
    tokens, width = acts.shape
    nz, nx = dp_size // 4, grp_size
    rows = width // (dp_size // 2 * nx)
    n_mat = width // LANES
    n_half = width // 2 // LANES
    n_all = n_mat + n_half
    even, odd = (n_all + 1) // 2, n_all // 2
    copies = n_all * (3 + 2 * (nx - 1) + 2 * (nz - 1) + 2)
    f32 = jnp.float32

    def room(*shape):
        return pltpu.VMEM(shape + (rows, LANES), f32)

    vmem = pl.BlockSpec(memory_space=pltpu.VMEM)
    return pl.pallas_call(
        functools.partial(reduce_kernel, nz, nx),
        out_shape=[
            jax.ShapeDtypeStruct((n_mat, nz, 2, nx, rows, LANES), f32),
            jax.ShapeDtypeStruct((n_half, 2, rows, LANES), f32),
        ],
        in_specs=[vmem, vmem],
        out_specs=[vmem, vmem],
        scratch_shapes=[
            pltpu.VMEM((2, tokens, width), acts.dtype),
            pltpu.VMEM((2, width, tokens), acts.dtype),
            room(n_all, nz, 2, nx),
            room(n_all, nz, 2, nx),
            room(n_all, nz, 2, nx),
            room(even, nz, 2),
            room(odd, nz, nx),
            room(even, nx - 1, nz, 2),
            room(even, nz),
            room(odd, nz, nx),
            room(odd, nx - 1, nz),
            room(n_all, nz),
            room(n_all, nz - 1),
            room(n_all),
            pltpu.SemaphoreType.DMA((copies,)),
            pltpu.SemaphoreType.DMA((copies,)),
        ],
        compiler_params=pltpu.CompilerParams(
            collective_id=0, has_side_effects=True, vmem_limit_bytes=60 * 1024 * 1024
        ),
    )(acts, grads)


def local(acts, grads, damping):
    dp_size = lax.axis_size("dp")
    grp_size = lax.axis_size("grp")
    core = lax.rem(lax.axis_index("dp"), 2)
    width = acts.shape[1]
    scale = 1.0 / (acts.shape[0] * dp_size * grp_size)
    mat, cross = reduce_grams(acts, grads, dp_size, grp_size)
    rows = cross.shape[2]
    chips = width // rows
    mat = jnp.moveaxis(mat.reshape(mat.shape[0], width, LANES), 0, 1).reshape(width, width)
    damp = jnp.where(core == 0, damping[0], damping[1])
    parts = factors(mat * scale + damp * jnp.eye(width, dtype=jnp.float32))
    cross = jnp.transpose(cross, (2, 1, 0, 3)).reshape(rows, width) * scale
    mapped = apply_inverse(cross, parts).T.reshape(dp_size // 2, 1, grp_size, rows, rows)
    mapped = jnp.broadcast_to(mapped, (dp_size // 2, 2, grp_size, rows, rows))
    mapped = lax.all_to_all(
        mapped.reshape(2 * chips, rows, rows), ("dp", "grp"), 0, 0, tiled=True
    )
    mapped = mapped.reshape(dp_size // 2, 2, grp_size, rows, rows)[:, 0]
    mapped = jnp.moveaxis(mapped.reshape(chips, rows, rows), 0, 1).reshape(rows, width)
    result = apply_inverse(mapped, parts)
    result = lax.all_to_all(result, "grp", 1, 0, tiled=True)
    out_rows = width // dp_size
    moved = lax.ppermute(result[:out_rows], "dp", [(i + 1, i) for i in range(0, dp_size, 2)])
    return jnp.where(core == 0, moved, result[out_rows:])


def solution(mesh):
    placed = (P(("dp", "grp"), None), P(("dp", "grp"), None), P())
    return jax.shard_map(
        local, mesh=mesh, in_specs=placed, out_specs=P("dp", "grp"), check_vma=False
    )
```

```python
import functools

import jax
import jax.numpy as jnp
from jax import lax
from jax.experimental import pallas as pl
from jax.experimental.pallas import tpu as pltpu
from jax.sharding import PartitionSpec as P

LANES = 128
PANEL = 256
MESH = pl.DeviceIdType.MESH


def kernel(
    nz, nx, scale, damping, acts, grads, out,
    mat, cross, stack, flipped, outgoing, incoming, own,
    sum_e, sum_o, got_e1, got_e2, got_o1, got_o2, pair, got_z, mine,
    full, high, low, block, wide, turned, landed, parted,
    send_sem, recv_sem, turn_send, turn_recv, part_send, part_recv,
):
    dp = lax.axis_index("dp")
    x = lax.axis_index("grp")
    core = lax.rem(dp, 2)
    y = lax.rem(dp // 2, 2)
    z = dp // 4
    other = 1 - core
    width = acts.shape[1]
    tiles = width // LANES
    n_mat = tiles // 2 + 1
    n_all = n_mat + tiles // 2
    half = width // 2
    rows = own.shape[-2]
    chips = width // rows
    chip = dp // 2 * nx + x

    def at(zz, yy, cc, xx):
        return ((zz * 2 + yy) * 2 + cc, xx)

    partner = at(z, y, other, x)
    y_peer = at(z, 1 - y, core, x)
    x_ids = [lax.rem(x + o, nx) for o in range(1, nx)]
    z_ids = [lax.rem(z + o, nz) for o in range(1, nz)]
    x_peers = [at(z, y, core, i) for i in x_ids]
    z_peers = [at(i, y, core, x) for i in z_ids]
    spread = [
        at(i // nx // 2, i // nx % 2, other, i % nx) for i in range(chips)
    ]
    peers = [y_peer] + x_peers + z_peers + spread

    barrier = pltpu.get_barrier_semaphore()
    for peer in peers:
        pl.semaphore_signal(barrier, inc=1, device_id=peer, device_id_type=MESH)
    pl.semaphore_wait(barrier, len(peers))

    count = [0]
    copies = []

    def send(src, dst, peer):
        n = count[0]
        count[0] += 1
        copy = pltpu.make_async_remote_copy(
            src_ref=src, dst_ref=dst, send_sem=send_sem.at[n], recv_sem=recv_sem.at[n],
            device_id=peer, device_id_type=MESH,
        )
        copy.start()
        copies.append(copy)
        return copy

    stack[0] = acts[...]
    stack[1] = grads[...]
    flipped[0] = acts[...].T
    flipped[1] = grads[...].T

    def term(role, chunk):
        if chunk < n_mat:
            pieces = []
            for i in range(tiles):
                j = (i + chunk) % tiles
                pieces.append(jnp.dot(
                    flipped[role, i * LANES:(i + 1) * LANES, :],
                    stack[role, :, j * LANES:(j + 1) * LANES],
                    preferred_element_type=jnp.float32,
                ))
            value = jnp.concatenate(pieces, axis=0)
        else:
            start = pl.multiple_of(role * half + (chunk - n_mat) * LANES, LANES)
            value = jnp.dot(
                flipped[1], stack[0, :, pl.ds(start, LANES)], preferred_element_type=jnp.float32
            )
        return value.reshape(own.shape[1:])

    waits = {}

    def core_send(c):
        outgoing[c] = term(other, c)
        waits[c] = [send(outgoing.at[c], incoming.at[c], partner)]
        own[c] = term(core, c)

    def arrived(c):
        for copy in waits[c]:
            copy.wait_recv()

    def first(c):
        arrived(c)
        own[c] = own[c] + incoming[c]
        k = c // 2
        if c % 2 == 0:
            waits[c] = [
                send(own.at[c, :, :, i], got_e1.at[k, s], peer)
                for s, (i, peer) in enumerate(zip(x_ids, x_peers))
            ]
        else:
            waits[c] = [send(own.at[c, :, 1 - y], got_o1.at[k], y_peer)]

    def second(c):
        arrived(c)
        k = c // 2
        if c % 2 == 0:
            total = own[c, :, :, x]
            for s in range(nx - 1):
                total = total + got_e1[k, s]
            sum_e[k] = total
            waits[c] = [send(sum_e.at[k, :, 1 - y], got_e2.at[k], y_peer)]
        else:
            sum_o[k] = own[c, :, y] + got_o1[k]
            waits[c] = [
                send(sum_o.at[k, :, i], got_o2.at[k, s], peer)
                for s, (i, peer) in enumerate(zip(x_ids, x_peers))
            ]

    def third(c):
        arrived(c)
        k = c // 2
        if c % 2 == 0:
            pair[c] = sum_e[k, :, y] + got_e2[k]
        else:
            total = sum_o[k, :, x]
            for s in range(nx - 1):
                total = total + got_o2[k, s]
            pair[c] = total
        waits[c] = [
            send(pair.at[c, i], got_z.at[c, s], peer)
            for s, (i, peer) in enumerate(zip(z_ids, z_peers))
        ]

    def fourth(c):
        arrived(c)
        total = pair[c, z]
        for s in range(nz - 1):
            total = total + got_z[c, s]
        mine[c] = total
        if c < n_mat:
            mat[c, z, y, x] = total
            spot = mat.at[c, z, y, x]
            waits[c] = [send(mine.at[c], spot, peer) for peer in z_peers]
        else:
            cross[c - n_mat, core] = total
            waits[c] = [send(mine.at[c], cross.at[c - n_mat, core], partner)]

    def fifth(c):
        arrived(c)
        if c >= n_mat:
            waits[c] = []
        elif c % 2 == 0:
            spot = mat.at[c, :, y, x]
            waits[c] = [send(spot, spot, y_peer)]
        else:
            spot = mat.at[c, :, y, x]
            waits[c] = [send(spot, spot, peer) for peer in x_peers]

    def sixth(c):
        arrived(c)
        if c >= n_mat:
            waits[c] = []
        elif c % 2 == 0:
            spot = mat.at[c, :, :, x]
            waits[c] = [send(spot, spot, peer) for peer in x_peers]
        else:
            spot = mat.at[c, :, y]
            waits[c] = [send(spot, spot, y_peer)]

    steps = [core_send, first, second, third, fourth, fifth, sixth, arrived]
    lag = 2
    for t in range(n_all + lag * len(steps)):
        for s, step in enumerate(steps):
            c = t - lag * s
            if 0 <= c < n_all:
                step(c)
    corner = (
        lax.broadcasted_iota(jnp.int32, (LANES, LANES), 0)
        == lax.broadcasted_iota(jnp.int32, (LANES, LANES), 1)
    ).astype(jnp.float32)
    damp = damping[core]

    def tile(i):
        return slice(i * LANES, (i + 1) * LANES)

    for c in range(n_mat):
        value = mat[c].reshape(width, LANES) * scale
        for i in range(tiles):
            piece = value[tile(i)]
            if c == 0:
                piece = piece + damp * corner
            j = (i + c) % tiles
            full[tile(i), tile(j)] = piece
            if 0 < c < tiles // 2:
                full[tile(j), tile(i)] = piece.T
    largest = jnp.max(jnp.sum(jnp.abs(full[...]), axis=0, keepdims=True), axis=1, keepdims=True)
    alpha = 1.0 / largest

    def parts(value):
        top = value.astype(jnp.bfloat16)
        return top, (value - top.astype(jnp.float32)).astype(jnp.bfloat16)

    for i in range(tiles):
        ids = lax.broadcasted_iota(jnp.int32, (LANES, width), 0) + i * LANES
        unit = (ids == lax.broadcasted_iota(jnp.int32, (LANES, width), 1)).astype(jnp.float32)
        high[0, tile(i)], low[0, tile(i)] = parts(unit - alpha * full[tile(i)])

    def mul(left, right):
        return jnp.dot(left, right, preferred_element_type=jnp.float32)

    @pl.loop(0, 2 * (width // PANEL))
    def _(n):
        k = n // (width // PANEL)
        cols = pl.ds(pl.multiple_of(lax.rem(n, width // PANEL) * PANEL, PANEL), PANEL)
        value = mul(low[k], high[k, :, cols]) + mul(high[k], low[k, :, cols])
        value = value + mul(high[k], high[k, :, cols])
        high[k + 1, :, cols], low[k + 1, :, cols] = parts(value)

    def apply_inverse():
        block[1] = block[0]

        @pl.loop(0, 5)
        def _(k):
            power = jnp.minimum(k, 2)
            value = block[1]
            top = value.astype(jnp.bfloat16).astype(jnp.float32)
            wide[...] = jnp.concatenate([top, value - top], axis=0).astype(jnp.bfloat16)

            @pl.loop(0, width // PANEL)
            def _(n):
                cols = pl.ds(pl.multiple_of(n * PANEL, PANEL), PANEL)
                both = mul(wide[...], high[power, :, cols])
                rest = mul(wide[...], low[power, :, cols])
                block[1, :, cols] = both[:rows] + (both[rows:] + rest[:rows])

            @pl.when(k != 3)
            def _():
                block[0] = block[0] + block[1]

            @pl.when(k < 3)
            def _():
                block[1] = block[0]

        block[0] = alpha * block[0]

    for c in range(n_all - n_mat):
        for h in range(2):
            start = h * half + c * LANES
            block[0, :, start:start + LANES] = cross[c, h] * scale
    apply_inverse()

    turned[...] = block[0].T.reshape(chips, rows, rows)
    turns = []
    for i, peer in enumerate(spread):
        turns.append(pltpu.make_async_remote_copy(
            src_ref=turned.at[i], dst_ref=landed.at[chip], send_sem=turn_send.at[i],
            recv_sem=turn_recv.at[chip], device_id=peer, device_id_type=MESH,
        ))
        turns[-1].start()
    for i in range(chips):
        pltpu.make_async_remote_copy(
            src_ref=turned.at[i], dst_ref=landed.at[i], send_sem=turn_send.at[i],
            recv_sem=turn_recv.at[i], device_id=spread[i], device_id_type=MESH,
        ).wait_recv()
    for i in range(chips):
        block[0, :, i * rows:(i + 1) * rows] = landed[i]
    apply_inverse()

    share = nx // 2
    span = width // nx
    slot = lax.rem(x, share)
    home = x // share

    for i in range(nx):
        parted[i] = block[0, :, i * span:(i + 1) * span]

    def part(o, where):
        i = lax.rem(x + o, nx)
        return pltpu.make_async_remote_copy(
            src_ref=parted.at[i], dst_ref=out.at[where], send_sem=part_send.at[o],
            recv_sem=part_recv.at[where], device_id=at(z, y, home if o else 0, i),
            device_id_type=MESH,
        )

    @pl.when(core == 1)
    def _():
        for o in range(1, nx):
            part(o, slot).start()

        @pl.when(home == 0)
        def _():
            part(0, slot).start()

        @pl.when(home == 1)
        def _():
            out[slot] = parted[x]

    for s in range(share):
        @pl.when(jnp.logical_or(core == 0, x != share + s))
        def _():
            part(1, s).wait_recv()

    @pl.when(core == 1)
    def _():
        for o in range(1, nx):
            part(o, slot).wait_send()

        @pl.when(home == 0)
        def _():
            part(0, slot).wait_send()

    for copy in copies + turns:
        copy.wait_send()


def local(acts, grads, damping):
    nz = lax.axis_size("dp") // 4
    nx = lax.axis_size("grp")
    tokens, width = acts.shape
    chips = 2 * nz * nx
    rows = width // chips
    tiles = width // LANES
    n_mat = tiles // 2 + 1
    n_half = tiles // 2
    n_all = n_mat + n_half
    even, odd = (n_all + 1) // 2, n_all // 2
    copies = n_all * (3 + 2 * (nx - 1) + 2 * (nz - 1) + 2)
    f32, bf16 = jnp.float32, jnp.bfloat16

    def room(*shape):
        return pltpu.VMEM(shape + (rows, LANES), f32)

    vmem = pl.BlockSpec(memory_space=pltpu.VMEM)
    out = pl.pallas_call(
        functools.partial(kernel, nz, nx, 1.0 / (tokens * 2 * chips)),
        out_shape=jax.ShapeDtypeStruct((nx // 2, rows, width // nx), f32),
        in_specs=[pl.BlockSpec(memory_space=pltpu.SMEM), vmem, vmem],
        out_specs=vmem,
        scratch_shapes=[
            room(n_mat, nz, 2, nx),
            room(n_half, 2),
            pltpu.VMEM((2, tokens, width), bf16),
            pltpu.VMEM((2, width, tokens), bf16),
            room(n_all, nz, 2, nx),
            room(n_all, nz, 2, nx),
            room(n_all, nz, 2, nx),
            room(even, nz, 2),
            room(odd, nz, nx),
            room(even, nx - 1, nz, 2),
            room(even, nz),
            room(odd, nz, nx),
            room(odd, nx - 1, nz),
            room(n_all, nz),
            room(n_all, nz - 1),
            room(n_all),
            pltpu.VMEM((width, width), f32),
            pltpu.VMEM((3, width, width), bf16),
            pltpu.VMEM((3, width, width), bf16),
            pltpu.VMEM((2, rows, width), f32),
            pltpu.VMEM((2 * rows, width), bf16),
            pltpu.VMEM((chips, rows, rows), f32),
            pltpu.VMEM((chips, rows, rows), f32),
            pltpu.VMEM((nx, rows, width // nx), f32),
            pltpu.SemaphoreType.DMA((copies,)),
            pltpu.SemaphoreType.DMA((copies,)),
            pltpu.SemaphoreType.DMA((chips,)),
            pltpu.SemaphoreType.DMA((chips,)),
            pltpu.SemaphoreType.DMA((nx,)),
            pltpu.SemaphoreType.DMA((nx // 2,)),
        ],
        compiler_params=pltpu.CompilerParams(
            collective_id=0, has_side_effects=True, vmem_limit_bytes=62 * 1024 * 1024
        ),
    )(damping, acts, grads)
    return out.reshape(nx // 2 * rows, width // nx)


def solution(mesh):
    placed = (P(("dp", "grp"), None), P(("dp", "grp"), None), P())
    return jax.shard_map(
        local, mesh=mesh, in_specs=placed, out_specs=P("dp", "grp"), check_vma=False
    )
```

```python
import functools

import jax
import jax.numpy as jnp
from jax import lax
from jax.experimental import pallas as pl
from jax.experimental.pallas import tpu as pltpu
from jax.sharding import PartitionSpec as P

LANES = 128
PANEL = 256
MESH = pl.DeviceIdType.MESH


def kernel(
    nz, nx, scale, damping, acts, grads, out,
    mat, cross, stack, flipped, outgoing, incoming, own,
    sum_e, sum_o, got_e1, got_e2, got_o1, got_o2, pair, got_z, mine,
    full, high, low, block, wide, turned, landed, parted,
    send_sem, recv_sem, turn_send, turn_recv, part_send, part_recv,
):
    dp = lax.axis_index("dp")
    x = lax.axis_index("grp")
    core = lax.rem(dp, 2)
    y = lax.rem(dp // 2, 2)
    z = dp // 4
    other = 1 - core
    width = acts.shape[1]
    tiles = width // LANES
    n_mat = tiles // 2 + 1
    n_all = n_mat + tiles // 2
    half = width // 2
    rows = own.shape[-2]
    chips = width // rows
    chip = dp // 2 * nx + x

    def at(zz, yy, cc, xx):
        return ((zz * 2 + yy) * 2 + cc, xx)

    partner = at(z, y, other, x)
    y_peer = at(z, 1 - y, core, x)
    x_ids = [lax.rem(x + o, nx) for o in range(1, nx)]
    z_ids = [lax.rem(z + o, nz) for o in range(1, nz)]
    x_peers = [at(z, y, core, i) for i in x_ids]
    z_peers = [at(i, y, core, x) for i in z_ids]
    spread = [
        at(i // nx // 2, i // nx % 2, other, i % nx) for i in range(chips)
    ]
    peers = [y_peer] + x_peers + z_peers + spread

    barrier = pltpu.get_barrier_semaphore()
    for peer in peers:
        pl.semaphore_signal(barrier, inc=1, device_id=peer, device_id_type=MESH)
    pl.semaphore_wait(barrier, len(peers))

    count = [0]
    copies = []

    def send(src, dst, peer):
        n = count[0]
        count[0] += 1
        copy = pltpu.make_async_remote_copy(
            src_ref=src, dst_ref=dst, send_sem=send_sem.at[n], recv_sem=recv_sem.at[n],
            device_id=peer, device_id_type=MESH,
        )
        copy.start()
        copies.append(copy)
        return copy

    stack[0] = acts[...]
    stack[1] = grads[...]
    flipped[0] = acts[...].T
    flipped[1] = grads[...].T

    def term(role, chunk):
        if chunk < n_mat:
            pieces = []
            for i in range(tiles):
                j = (i + chunk) % tiles
                pieces.append(jnp.dot(
                    flipped[role, i * LANES:(i + 1) * LANES, :],
                    stack[role, :, j * LANES:(j + 1) * LANES],
                    preferred_element_type=jnp.float32,
                ))
            value = jnp.concatenate(pieces, axis=0)
        else:
            start = pl.multiple_of(role * half + (chunk - n_mat) * LANES, LANES)
            value = jnp.dot(
                flipped[1], stack[0, :, pl.ds(start, LANES)], preferred_element_type=jnp.float32
            )
        return value.reshape(own.shape[1:])

    waits = {}

    def core_send(c):
        outgoing[c] = term(other, c)
        waits[c] = [send(outgoing.at[c], incoming.at[c], partner)]
        own[c] = term(core, c)

    def arrived(c):
        for copy in waits[c]:
            copy.wait_recv()

    def first(c):
        arrived(c)
        own[c] = own[c] + incoming[c]
        k = c // 2
        if c % 2 == 0:
            waits[c] = [
                send(own.at[c, :, :, i], got_e1.at[k, s], peer)
                for s, (i, peer) in enumerate(zip(x_ids, x_peers))
            ]
        else:
            waits[c] = [send(own.at[c, :, 1 - y], got_o1.at[k], y_peer)]

    def second(c):
        arrived(c)
        k = c // 2
        if c % 2 == 0:
            total = own[c, :, :, x]
            for s in range(nx - 1):
                total = total + got_e1[k, s]
            sum_e[k] = total
            waits[c] = [send(sum_e.at[k, :, 1 - y], got_e2.at[k], y_peer)]
        else:
            sum_o[k] = own[c, :, y] + got_o1[k]
            waits[c] = [
                send(sum_o.at[k, :, i], got_o2.at[k, s], peer)
                for s, (i, peer) in enumerate(zip(x_ids, x_peers))
            ]

    def third(c):
        arrived(c)
        k = c // 2
        if c % 2 == 0:
            pair[c] = sum_e[k, :, y] + got_e2[k]
        else:
            total = sum_o[k, :, x]
            for s in range(nx - 1):
                total = total + got_o2[k, s]
            pair[c] = total
        waits[c] = [
            send(pair.at[c, i], got_z.at[c, s], peer)
            for s, (i, peer) in enumerate(zip(z_ids, z_peers))
        ]

    def fourth(c):
        arrived(c)
        total = pair[c, z]
        for s in range(nz - 1):
            total = total + got_z[c, s]
        mine[c] = total
        if c < n_mat:
            mat[c, z, y, x] = total
            spot = mat.at[c, z, y, x]
            waits[c] = [send(mine.at[c], spot, peer) for peer in z_peers]
        else:
            cross[c - n_mat, core] = total
            waits[c] = [send(mine.at[c], cross.at[c - n_mat, core], partner)]

    def fifth(c):
        arrived(c)
        if c >= n_mat:
            waits[c] = []
        elif c % 2 == 0:
            spot = mat.at[c, :, y, x]
            waits[c] = [send(spot, spot, y_peer)]
        else:
            spot = mat.at[c, :, y, x]
            waits[c] = [send(spot, spot, peer) for peer in x_peers]

    def sixth(c):
        arrived(c)
        if c >= n_mat:
            waits[c] = []
        elif c % 2 == 0:
            spot = mat.at[c, :, :, x]
            waits[c] = [send(spot, spot, peer) for peer in x_peers]
        else:
            spot = mat.at[c, :, y]
            waits[c] = [send(spot, spot, y_peer)]

    corner = (
        lax.broadcasted_iota(jnp.int32, (LANES, LANES), 0)
        == lax.broadcasted_iota(jnp.int32, (LANES, LANES), 1)
    ).astype(jnp.float32)
    damp = damping[core]

    def tile(i):
        return slice(i * LANES, (i + 1) * LANES)

    def unpack(c):
        arrived(c)
        value = mat[c].reshape(width, LANES) * scale
        for i in range(tiles):
            piece = value[tile(i)]
            if c == 0:
                piece = piece + damp * corner
            j = (i + c) % tiles
            full[tile(i), tile(j)] = piece
            if 0 < c < tiles // 2:
                full[tile(j), tile(i)] = piece.T

    steps = [core_send, first, second, third, fourth, fifth, sixth, unpack]
    lag = 2
    late = lag * 6 + 1
    for t in range(n_mat + lag * len(steps)):
        for s, step in enumerate(steps):
            c = t - lag * s
            if 0 <= c < n_mat:
                step(c)
        if n_mat <= t < n_all:
            core_send(t)
        if late <= t < late + n_all - n_mat:
            first(t - late + n_mat)

    largest = jnp.max(jnp.sum(jnp.abs(full[...]), axis=0, keepdims=True), axis=1, keepdims=True)
    alpha = 1.0 / largest

    def parts(value):
        top = value.astype(jnp.bfloat16)
        return top, (value - top.astype(jnp.float32)).astype(jnp.bfloat16)

    for i in range(tiles):
        ids = lax.broadcasted_iota(jnp.int32, (LANES, width), 0) + i * LANES
        unit = (ids == lax.broadcasted_iota(jnp.int32, (LANES, width), 1)).astype(jnp.float32)
        high[0, tile(i)], low[0, tile(i)] = parts(unit - alpha * full[tile(i)])

    def mul(left, right):
        return jnp.dot(left, right, preferred_element_type=jnp.float32)

    pending = [(step, c) for step in (second, third, fourth) for c in range(n_mat, n_all)]
    panels = 2 * (width // PANEL)
    for n in range(panels):
        k, start = n // (width // PANEL), n % (width // PANEL) * PANEL
        stop = start + PANEL
        cols, below = slice(start, stop), slice(start, width)
        value = mul(low[k, below], high[k, :, cols]) + mul(high[k, below], low[k, :, cols])
        value = value + mul(high[k, below], high[k, :, cols])
        top, rest = parts(value)
        high[k + 1, below, cols], low[k + 1, below, cols] = top, rest
        if stop < width:
            high[k + 1, cols, stop:] = top[PANEL:].T
            low[k + 1, cols, stop:] = rest[PANEL:].T
        taken = -(-len(pending) // max(panels - 1 - n, 1))
        for step, c in pending[:taken]:
            step(c)
        pending = pending[taken:]
    for c in range(n_mat, n_all):
        arrived(c)

    def apply_inverse():
        block[1] = block[0]

        @pl.loop(0, 5)
        def _(k):
            power = jnp.minimum(k, 2)
            value = block[1]
            top = value.astype(jnp.bfloat16).astype(jnp.float32)
            wide[...] = jnp.concatenate([top, value - top], axis=0).astype(jnp.bfloat16)

            @pl.loop(0, width // PANEL)
            def _(n):
                cols = pl.ds(pl.multiple_of(n * PANEL, PANEL), PANEL)
                both = mul(wide[...], high[power, :, cols])
                rest = mul(wide[...], low[power, :, cols])
                block[1, :, cols] = both[:rows] + (both[rows:] + rest[:rows])

            @pl.when(k != 3)
            def _():
                block[0] = block[0] + block[1]

            @pl.when(k < 3)
            def _():
                block[1] = block[0]

        block[0] = alpha * block[0]

    for c in range(n_all - n_mat):
        for h in range(2):
            start = h * half + c * LANES
            block[0, :, start:start + LANES] = cross[c, h] * scale
    apply_inverse()

    turned[...] = block[0].T.reshape(chips, rows, rows)
    turns = []
    for i, peer in enumerate(spread):
        turns.append(pltpu.make_async_remote_copy(
            src_ref=turned.at[i], dst_ref=landed.at[chip], send_sem=turn_send.at[i],
            recv_sem=turn_recv.at[chip], device_id=peer, device_id_type=MESH,
        ))
        turns[-1].start()
    for i in range(chips):
        pltpu.make_async_remote_copy(
            src_ref=turned.at[i], dst_ref=landed.at[i], send_sem=turn_send.at[i],
            recv_sem=turn_recv.at[i], device_id=spread[i], device_id_type=MESH,
        ).wait_recv()
    for i in range(chips):
        block[0, :, i * rows:(i + 1) * rows] = landed[i]
    apply_inverse()

    share = nx // 2
    span = width // nx
    slot = lax.rem(x, share)
    home = x // share

    for i in range(nx):
        parted[i] = block[0, :, i * span:(i + 1) * span]

    def part(o, where):
        i = lax.rem(x + o, nx)
        return pltpu.make_async_remote_copy(
            src_ref=parted.at[i], dst_ref=out.at[where], send_sem=part_send.at[o],
            recv_sem=part_recv.at[where], device_id=at(z, y, home if o else 0, i),
            device_id_type=MESH,
        )

    @pl.when(core == 1)
    def _():
        for o in range(1, nx):
            part(o, slot).start()

        @pl.when(home == 0)
        def _():
            part(0, slot).start()

        @pl.when(home == 1)
        def _():
            out[slot] = parted[x]

    for s in range(share):
        @pl.when(jnp.logical_or(core == 0, x != share + s))
        def _():
            part(1, s).wait_recv()

    @pl.when(core == 1)
    def _():
        for o in range(1, nx):
            part(o, slot).wait_send()

        @pl.when(home == 0)
        def _():
            part(0, slot).wait_send()

    for copy in copies + turns:
        copy.wait_send()


def local(acts, grads, damping):
    nz = lax.axis_size("dp") // 4
    nx = lax.axis_size("grp")
    tokens, width = acts.shape
    chips = 2 * nz * nx
    rows = width // chips
    tiles = width // LANES
    n_mat = tiles // 2 + 1
    n_half = tiles // 2
    n_all = n_mat + n_half
    even, odd = (n_all + 1) // 2, n_all // 2
    copies = n_all * (3 + 2 * (nx - 1) + 2 * (nz - 1) + 2)
    f32, bf16 = jnp.float32, jnp.bfloat16

    def room(*shape):
        return pltpu.VMEM(shape + (rows, LANES), f32)

    vmem = pl.BlockSpec(memory_space=pltpu.VMEM)
    out = pl.pallas_call(
        functools.partial(kernel, nz, nx, 1.0 / (tokens * 2 * chips)),
        out_shape=jax.ShapeDtypeStruct((nx // 2, rows, width // nx), f32),
        in_specs=[pl.BlockSpec(memory_space=pltpu.SMEM), vmem, vmem],
        out_specs=vmem,
        scratch_shapes=[
            room(n_mat, nz, 2, nx),
            room(n_half, 2),
            pltpu.VMEM((2, tokens, width), bf16),
            pltpu.VMEM((2, width, tokens), bf16),
            room(n_all, nz, 2, nx),
            room(n_all, nz, 2, nx),
            room(n_all, nz, 2, nx),
            room(even, nz, 2),
            room(odd, nz, nx),
            room(even, nx - 1, nz, 2),
            room(even, nz),
            room(odd, nz, nx),
            room(odd, nx - 1, nz),
            room(n_all, nz),
            room(n_all, nz - 1),
            room(n_all),
            pltpu.VMEM((width, width), f32),
            pltpu.VMEM((3, width, width), bf16),
            pltpu.VMEM((3, width, width), bf16),
            pltpu.VMEM((2, rows, width), f32),
            pltpu.VMEM((2 * rows, width), bf16),
            pltpu.VMEM((chips, rows, rows), f32),
            pltpu.VMEM((chips, rows, rows), f32),
            pltpu.VMEM((nx, rows, width // nx), f32),
            pltpu.SemaphoreType.DMA((copies,)),
            pltpu.SemaphoreType.DMA((copies,)),
            pltpu.SemaphoreType.DMA((chips,)),
            pltpu.SemaphoreType.DMA((chips,)),
            pltpu.SemaphoreType.DMA((nx,)),
            pltpu.SemaphoreType.DMA((nx // 2,)),
        ],
        compiler_params=pltpu.CompilerParams(
            collective_id=0, has_side_effects=True, vmem_limit_bytes=62 * 1024 * 1024
        ),
    )(damping, acts, grads)
    return out.reshape(nx // 2 * rows, width // nx)


def solution(mesh):
    placed = (P(("dp", "grp"), None), P(("dp", "grp"), None), P())
    return jax.shard_map(
        local, mesh=mesh, in_specs=placed, out_specs=P("dp", "grp"), check_vma=False
    )
```

```python
import functools

import jax
import jax.numpy as jnp
from jax import lax
from jax.experimental import pallas as pl
from jax.experimental.pallas import tpu as pltpu
from jax.sharding import PartitionSpec as P

LANES = 128
PANEL = 256
MESH = pl.DeviceIdType.MESH


def kernel(
    nz, nx, scale, damping, acts, grads, out,
    mat, cross, stack, flipped, outgoing, incoming, own,
    sum_e, sum_o, got_e1, got_e2, got_o1, got_o2, pair, got_z, mine,
    full, high, low, block, wide, turned, landed, parted,
    send_sem, recv_sem, turn_send, turn_recv, part_send, part_recv,
):
    dp = lax.axis_index("dp")
    x = lax.axis_index("grp")
    core = lax.rem(dp, 2)
    y = lax.rem(dp // 2, 2)
    z = dp // 4
    other = 1 - core
    width = acts.shape[1]
    tiles = width // LANES
    n_mat = tiles // 2 + 1
    n_all = n_mat + tiles // 2
    half = width // 2
    rows = own.shape[-2]
    chips = width // rows
    chip = dp // 2 * nx + x

    def at(zz, yy, cc, xx):
        return ((zz * 2 + yy) * 2 + cc, xx)

    partner = at(z, y, other, x)
    y_peer = at(z, 1 - y, core, x)
    x_ids = [lax.rem(x + o, nx) for o in range(1, nx)]
    z_ids = [lax.rem(z + o, nz) for o in range(1, nz)]
    x_peers = [at(z, y, core, i) for i in x_ids]
    z_peers = [at(i, y, core, x) for i in z_ids]
    spread = [
        at(i // nx // 2, i // nx % 2, other, i % nx) for i in range(chips)
    ]
    peers = [y_peer] + x_peers + z_peers + spread

    barrier = pltpu.get_barrier_semaphore()
    for peer in peers:
        pl.semaphore_signal(barrier, inc=1, device_id=peer, device_id_type=MESH)
    pl.semaphore_wait(barrier, len(peers))

    count = [0]
    copies = []

    def send(src, dst, peer):
        n = count[0]
        count[0] += 1
        copy = pltpu.make_async_remote_copy(
            src_ref=src, dst_ref=dst, send_sem=send_sem.at[n], recv_sem=recv_sem.at[n],
            device_id=peer, device_id_type=MESH,
        )
        copy.start()
        copies.append(copy)
        return copy

    stack[0] = acts[...]
    stack[1] = grads[...]
    flipped[0] = acts[...].T
    flipped[1] = grads[...].T

    def term(role, chunk):
        if chunk < n_mat:
            pieces = []
            for i in range(tiles):
                j = (i + chunk) % tiles
                pieces.append(jnp.dot(
                    flipped[role, i * LANES:(i + 1) * LANES, :],
                    stack[role, :, j * LANES:(j + 1) * LANES],
                    preferred_element_type=jnp.float32,
                ))
            value = jnp.concatenate(pieces, axis=0)
        else:
            start = pl.multiple_of(role * half + (chunk - n_mat) * LANES, LANES)
            value = jnp.dot(
                flipped[1], stack[0, :, pl.ds(start, LANES)], preferred_element_type=jnp.float32
            )
        return value.reshape(own.shape[1:])

    waits = {}

    def core_send(c):
        outgoing[c] = term(other, c)
        waits[c] = [send(outgoing.at[c], incoming.at[c], partner)]
        own[c] = term(core, c)

    def arrived(c):
        for copy in waits[c]:
            copy.wait_recv()

    def first(c):
        arrived(c)
        own[c] = own[c] + incoming[c]
        k = c // 2
        if c % 2 == 0:
            waits[c] = [
                send(own.at[c, :, :, i], got_e1.at[k, s], peer)
                for s, (i, peer) in enumerate(zip(x_ids, x_peers))
            ]
        else:
            waits[c] = [send(own.at[c, :, 1 - y], got_o1.at[k], y_peer)]

    def second(c):
        arrived(c)
        k = c // 2
        if c % 2 == 0:
            total = own[c, :, :, x]
            for s in range(nx - 1):
                total = total + got_e1[k, s]
            sum_e[k] = total
            waits[c] = [send(sum_e.at[k, :, 1 - y], got_e2.at[k], y_peer)]
        else:
            sum_o[k] = own[c, :, y] + got_o1[k]
            waits[c] = [
                send(sum_o.at[k, :, i], got_o2.at[k, s], peer)
                for s, (i, peer) in enumerate(zip(x_ids, x_peers))
            ]

    def third(c):
        arrived(c)
        k = c // 2
        if c % 2 == 0:
            pair[c] = sum_e[k, :, y] + got_e2[k]
        else:
            total = sum_o[k, :, x]
            for s in range(nx - 1):
                total = total + got_o2[k, s]
            pair[c] = total
        waits[c] = [
            send(pair.at[c, i], got_z.at[c, s], peer)
            for s, (i, peer) in enumerate(zip(z_ids, z_peers))
        ]

    def fourth(c):
        arrived(c)
        total = pair[c, z]
        for s in range(nz - 1):
            total = total + got_z[c, s]
        mine[c] = total
        if c < n_mat:
            mat[c, z, y, x] = total
            spot = mat.at[c, z, y, x]
            waits[c] = [send(mine.at[c], spot, peer) for peer in z_peers]
        else:
            cross[c - n_mat, core] = total
            waits[c] = [send(mine.at[c], cross.at[c - n_mat, core], partner)]

    def fifth(c):
        arrived(c)
        if c >= n_mat:
            waits[c] = []
        elif c % 2 == 0:
            spot = mat.at[c, :, y, x]
            waits[c] = [send(spot, spot, y_peer)]
        else:
            spot = mat.at[c, :, y, x]
            waits[c] = [send(spot, spot, peer) for peer in x_peers]

    def sixth(c):
        arrived(c)
        if c >= n_mat:
            waits[c] = []
        elif c % 2 == 0:
            spot = mat.at[c, :, :, x]
            waits[c] = [send(spot, spot, peer) for peer in x_peers]
        else:
            spot = mat.at[c, :, y]
            waits[c] = [send(spot, spot, y_peer)]

    steps = [core_send, first, second, third, fourth, fifth, sixth, arrived]
    lag = 2
    for t in range(n_all + lag * len(steps)):
        for s, step in enumerate(steps):
            c = t - lag * s
            if 0 <= c < n_all:
                step(c)
    corner = (
        lax.broadcasted_iota(jnp.int32, (LANES, LANES), 0)
        == lax.broadcasted_iota(jnp.int32, (LANES, LANES), 1)
    ).astype(jnp.float32)
    damp = damping[core]

    def tile(i):
        return slice(i * LANES, (i + 1) * LANES)

    for c in range(n_mat):
        value = mat[c].reshape(width, LANES) * scale
        for i in range(tiles):
            piece = value[tile(i)]
            if c == 0:
                piece = piece + damp * corner
            j = (i + c) % tiles
            full[tile(i), tile(j)] = piece
            if 0 < c < tiles // 2:
                full[tile(j), tile(i)] = piece.T
    largest = jnp.max(jnp.sum(jnp.abs(full[...]), axis=0, keepdims=True), axis=1, keepdims=True)
    alpha = 1.0 / largest

    def parts(value):
        top = value.astype(jnp.bfloat16)
        return top, (value - top.astype(jnp.float32)).astype(jnp.bfloat16)

    for i in range(tiles):
        ids = lax.broadcasted_iota(jnp.int32, (LANES, width), 0) + i * LANES
        unit = (ids == lax.broadcasted_iota(jnp.int32, (LANES, width), 1)).astype(jnp.float32)
        high[0, tile(i)], low[0, tile(i)] = parts(unit - alpha * full[tile(i)])

    def mul(left, right):
        return jnp.dot(left, right, preferred_element_type=jnp.float32)

    panels = 2 * (width // PANEL)
    for n in range(panels):
        k, start = n // (width // PANEL), n % (width // PANEL) * PANEL
        stop = start + PANEL
        cols, below = slice(start, stop), slice(start, width)
        value = mul(low[k, below], high[k, :, cols]) + mul(high[k, below], low[k, :, cols])
        value = value + mul(high[k, below], high[k, :, cols])
        top, rest = parts(value)
        high[k + 1, below, cols], low[k + 1, below, cols] = top, rest
        if stop < width:
            high[k + 1, cols, stop:] = top[PANEL:].T
            low[k + 1, cols, stop:] = rest[PANEL:].T

    def apply_inverse():
        block[1] = block[0]

        @pl.loop(0, 5)
        def _(k):
            power = jnp.minimum(k, 2)
            value = block[1]
            top = value.astype(jnp.bfloat16).astype(jnp.float32)
            wide[...] = jnp.concatenate([top, value - top], axis=0).astype(jnp.bfloat16)

            @pl.loop(0, width // PANEL)
            def _(n):
                cols = pl.ds(pl.multiple_of(n * PANEL, PANEL), PANEL)
                both = mul(wide[...], high[power, :, cols])
                rest = mul(wide[...], low[power, :, cols])
                block[1, :, cols] = both[:rows] + (both[rows:] + rest[:rows])

            @pl.when(k != 3)
            def _():
                block[0] = block[0] + block[1]

            @pl.when(k < 3)
            def _():
                block[1] = block[0]

        block[0] = alpha * block[0]

    for c in range(n_all - n_mat):
        for h in range(2):
            start = h * half + c * LANES
            block[0, :, start:start + LANES] = cross[c, h] * scale
    apply_inverse()

    turned[...] = block[0].T.reshape(chips, rows, rows)
    turns = []
    for i, peer in enumerate(spread):
        turns.append(pltpu.make_async_remote_copy(
            src_ref=turned.at[i], dst_ref=landed.at[chip], send_sem=turn_send.at[i],
            recv_sem=turn_recv.at[chip], device_id=peer, device_id_type=MESH,
        ))
        turns[-1].start()
    for i in range(chips):
        pltpu.make_async_remote_copy(
            src_ref=turned.at[i], dst_ref=landed.at[i], send_sem=turn_send.at[i],
            recv_sem=turn_recv.at[i], device_id=spread[i], device_id_type=MESH,
        ).wait_recv()
    for i in range(chips):
        block[0, :, i * rows:(i + 1) * rows] = landed[i]
    apply_inverse()

    share = nx // 2
    span = width // nx
    slot = lax.rem(x, share)
    home = x // share

    for i in range(nx):
        parted[i] = block[0, :, i * span:(i + 1) * span]

    def part(o, where):
        i = lax.rem(x + o, nx)
        return pltpu.make_async_remote_copy(
            src_ref=parted.at[i], dst_ref=out.at[where], send_sem=part_send.at[o],
            recv_sem=part_recv.at[where], device_id=at(z, y, home if o else 0, i),
            device_id_type=MESH,
        )

    @pl.when(core == 1)
    def _():
        for o in range(1, nx):
            part(o, slot).start()

        @pl.when(home == 0)
        def _():
            part(0, slot).start()

        @pl.when(home == 1)
        def _():
            out[slot] = parted[x]

    for s in range(share):
        @pl.when(jnp.logical_or(core == 0, x != share + s))
        def _():
            part(1, s).wait_recv()

    @pl.when(core == 1)
    def _():
        for o in range(1, nx):
            part(o, slot).wait_send()

        @pl.when(home == 0)
        def _():
            part(0, slot).wait_send()

    for copy in copies + turns:
        copy.wait_send()


def local(acts, grads, damping):
    nz = lax.axis_size("dp") // 4
    nx = lax.axis_size("grp")
    tokens, width = acts.shape
    chips = 2 * nz * nx
    rows = width // chips
    tiles = width // LANES
    n_mat = tiles // 2 + 1
    n_half = tiles // 2
    n_all = n_mat + n_half
    even, odd = (n_all + 1) // 2, n_all // 2
    copies = n_all * (3 + 2 * (nx - 1) + 2 * (nz - 1) + 2)
    f32, bf16 = jnp.float32, jnp.bfloat16

    def room(*shape):
        return pltpu.VMEM(shape + (rows, LANES), f32)

    vmem = pl.BlockSpec(memory_space=pltpu.VMEM)
    out = pl.pallas_call(
        functools.partial(kernel, nz, nx, 1.0 / (tokens * 2 * chips)),
        out_shape=jax.ShapeDtypeStruct((nx // 2, rows, width // nx), f32),
        in_specs=[pl.BlockSpec(memory_space=pltpu.SMEM), vmem, vmem],
        out_specs=vmem,
        scratch_shapes=[
            room(n_mat, nz, 2, nx),
            room(n_half, 2),
            pltpu.VMEM((2, tokens, width), bf16),
            pltpu.VMEM((2, width, tokens), bf16),
            room(n_all, nz, 2, nx),
            room(n_all, nz, 2, nx),
            room(n_all, nz, 2, nx),
            room(even, nz, 2),
            room(odd, nz, nx),
            room(even, nx - 1, nz, 2),
            room(even, nz),
            room(odd, nz, nx),
            room(odd, nx - 1, nz),
            room(n_all, nz),
            room(n_all, nz - 1),
            room(n_all),
            pltpu.VMEM((width, width), f32),
            pltpu.VMEM((3, width, width), bf16),
            pltpu.VMEM((3, width, width), bf16),
            pltpu.VMEM((2, rows, width), f32),
            pltpu.VMEM((2 * rows, width), bf16),
            pltpu.VMEM((chips, rows, rows), f32),
            pltpu.VMEM((chips, rows, rows), f32),
            pltpu.VMEM((nx, rows, width // nx), f32),
            pltpu.SemaphoreType.DMA((copies,)),
            pltpu.SemaphoreType.DMA((copies,)),
            pltpu.SemaphoreType.DMA((chips,)),
            pltpu.SemaphoreType.DMA((chips,)),
            pltpu.SemaphoreType.DMA((nx,)),
            pltpu.SemaphoreType.DMA((nx // 2,)),
        ],
        compiler_params=pltpu.CompilerParams(
            collective_id=0, has_side_effects=True, vmem_limit_bytes=62 * 1024 * 1024
        ),
    )(damping, acts, grads)
    return out.reshape(nx // 2 * rows, width // nx)


def solution(mesh):
    placed = (P(("dp", "grp"), None), P(("dp", "grp"), None), P())
    return jax.shard_map(
        local, mesh=mesh, in_specs=placed, out_specs=P("dp", "grp"), check_vma=False
    )
```
